32 devices in a mesh: fsdp: 8 (over y, x, core), tp: 4 (over z).
Axes of the slice: x: 2, y: 2, z: 4, core: 2. Of those that a mesh axis runs over, the one named last changes fastest.
Arguments:
- hidden_in: bfloat16 [8192, 2048], P(('fsdp', 'tp')), may hold values from -6 to 6
- seq_lengths: int32 [8], P('fsdp'), may hold values from 512 to 1024, as said below
- seq_offsets: int32 [8], P('fsdp'), may hold values from 0 to 512, as said below
- routes: int32 [8192, 8], P(('fsdp', 'tp')), may hold values from 0 to 15, all different within a row; in each aligned block of 256 rows (0 to 255, 256 to 511, ...) at most 144 rows name the same one
- attn_gain: float32 [2048], P('fsdp'), may hold values from 0.5 to 1.5
- w_query: float32 [2048, 2048], P('fsdp', 'tp'), may hold values from -0.125 to 0.125
- w_key: float32 [2048, 2048], P('fsdp', 'tp'), may hold values from -0.125 to 0.125
- w_value: float32 [2048, 2048], P('fsdp', 'tp'), may hold values from -0.125 to 0.125
- query_gain: float32 [128], P('fsdp'), may hold values from 0.5 to 1.5
- key_gain: float32 [128], P('fsdp'), may hold values from 0.5 to 1.5
- w_output: float32 [2048, 2048], P('tp', 'fsdp'), may hold values from -2 to 2
- ffn_gain: float32 [2048], P('fsdp'), may hold values from 0.5 to 1.5
- router: float32 [2048, 16], P('fsdp'), may hold values from -0.0625 to 0.0625
- w_gate: float32 [16, 2048, 1024], P('fsdp', None, 'tp'), may hold values from -0.125 to 0.125
- w_up: float32 [16, 2048, 1024], P('fsdp', None, 'tp'), may hold values from -0.125 to 0.125
- w_down: float32 [16, 1024, 2048], P('fsdp', 'tp'), may hold values from -2 to 2
- cotangent: float32 [8192, 2048], P(('fsdp', 'tp')), may hold values from -6 to 6
Outputs:
- block_out: bfloat16 [8192, 2048], P(('fsdp', 'tp'))
- grad_input: float32 [8192, 2048], P(('fsdp', 'tp'))
- grad_attn_gain: float32 [2048], P(('fsdp', 'tp'))
- grad_w_query: float32 [2048, 2048], P('fsdp', 'tp')
- grad_w_key: float32 [2048, 2048], P('fsdp', 'tp')
- grad_w_value: float32 [2048, 2048], P('fsdp', 'tp')
- grad_query_gain: float32 [128], P(('fsdp', 'tp'))
- grad_key_gain: float32 [128], P(('fsdp', 'tp'))
- grad_w_output: float32 [2048, 2048], P('tp', 'fsdp')
- grad_ffn_gain: float32 [2048], P(('fsdp', 'tp'))
- grad_router: float32 [2048, 16], P(('fsdp', 'tp'))
- grad_w_gate: float32 [16, 2048, 1024], P('fsdp', None, 'tp')
- grad_w_up: float32 [16, 2048, 1024], P('fsdp', None, 'tp')
- grad_w_down: float32 [16, 1024, 2048], P('fsdp', 'tp')
The draws below stay inside these ranges and needn't reach their ends.
Inputs may be any that keep to these rules, and one draw needn't show every extreme that they name: `seq_lengths`: real tokens of the sequence in each slot of 1024 rows; some slot is full and some slot is half full. `seq_offsets`: row within its slot at which each sequence starts; offset plus length is at most 1024. `routes`: each row names 8 different experts; among the rows of one device no expert is named more than 144 times, a bound that some block reaches.
All inputs are finite; a program needn't handle non-finite values.
Results may differ from the reference program's by a relative error of at most 0.025.
Values may be sent and summed in bfloat16 or wider, within the bound.
No kernel may reach another device: no remote copies, remote signals or barrier semaphores. Data moves between devices by JAX's collectives and lax.ppermute only.
A program may use at most 320 MiB of HBM per device.

```python
import math
import jax
import jax.numpy as jnp
import numpy as np
from jax import lax

D = 2048
H = 16
HD = 128
FF = 1024
TOP = 8
TOK_DEV = 256
EXPERTS = 16
GROUP = 1024
TOKENS = 8192
CAP = 144
N_FSDP = 8
N_TP = 4


def lengths_and_offsets(key):
    base_key = jax.random.fold_in(key, 11)
    drawn_lengths = jax.random.randint(jax.random.fold_in(base_key, 1), (N_FSDP,), GROUP // 2, GROUP + 1)
    chosen = jax.random.randint(jax.random.fold_in(base_key, 2), (), 0, N_FSDP)
    slot_ids = jnp.arange(N_FSDP)
    full_slot = slot_ids == chosen
    short_slot = slot_ids == (chosen + 1) % N_FSDP
    drawn_lengths = jnp.where(full_slot, GROUP, jnp.where(short_slot, GROUP // 2, drawn_lengths))
    spare_room = GROUP - drawn_lengths + 1
    raw_start = jax.random.randint(jax.random.fold_in(base_key, 3), (N_FSDP,), 0, GROUP)
    starts = jnp.where(short_slot, GROUP - GROUP // 2, raw_start % spare_room)
    return (drawn_lengths.astype(jnp.int32), starts.astype(jnp.int32))


def draw_seq_lengths(key, part):
    return lengths_and_offsets(key)[0]


def draw_seq_offsets(key, part):
    return lengths_and_offsets(key)[1]


def block_scale(own_key, dims, shards, smallest, high):
    level, own = 1.0, jax.random.fold_in(own_key, 6)
    for axis_at, shards_of in shards:
        steps = jnp.exp(jax.random.uniform(jax.random.fold_in(own, axis_at), (shards_of,), jnp.float32, smallest / len(shards), high / len(shards)))
        level = level * jnp.repeat(steps, dims[axis_at] // shards_of).reshape([-1 if axis == axis_at else 1 for axis in range(len(dims))])
    return level


def routed_block(rng, own, number, rows, count, top, most, slope):
    order = jax.random.permutation(rng, count)
    crowded, common = shares(count, rows * top, most, slope, True), shares(count, rows * top, most, slope, False)
    places = jnp.arange(count)

    def named(tallies, offset_by):
        used = int((tallies > 0).sum())
        fixed = max(1, used // 4)
        shifted = fixed + (places - fixed + offset_by * (used - fixed)) % max(1, count - fixed)
        return jnp.zeros((count,), jnp.int32).at[order[jnp.where(places < fixed, places, shifted)]].set(jnp.asarray(tallies, jnp.int32))

    tallies = jnp.where(number % 4 == 0, named(crowded, number // 4), named(common, number - number // 4 - 1))
    mixed = jax.random.permutation(jax.random.fold_in(own, 3), count)
    source_of, taker = mixed[0:count // 2 * 2:2], mixed[1:count // 2 * 2:2]
    room = jnp.minimum(tallies[source_of] - 1, most - tallies[taker]) // 2
    room = jnp.where((source_of == order[0]) | (taker == order[0]) | (tallies[taker] == 0), 0, jnp.maximum(room, 0))
    shifted = jax.random.randint(jax.random.fold_in(own, 4), (count // 2,), 0, 1 << 20) % (room + 1)
    tallies = tallies.at[source_of].add(-shifted).at[taker].add(shifted)
    items = jnp.searchsorted(jnp.cumsum(tallies), jnp.arange(rows * top), side="right").astype(jnp.int32)
    grid = items.reshape(top, rows).T
    grid = grid[jax.random.permutation(jax.random.fold_in(own, 1), rows)]
    offset_by = jax.random.randint(jax.random.fold_in(own, 2), (rows, 1), 0, top)
    return jnp.take_along_axis(grid, (jnp.arange(top)[None, :] + offset_by) % top, axis=1)


def shares(amount, total, limit, skew, full):
    weights = [(1 << 20) // math.isqrt(standing ** skew) + 1 for standing in range(1, amount + 1)]
    largest = limit if full else min(limit, max(-(-total // amount), total * weights[0] // sum(weights)))
    least = 1 if total - largest >= amount - 1 else 0
    counts, spare = [largest] + [least] * (amount - 1), total - largest - least * (amount - 1)
    while spare > 0:
        free = [i for i in range(1, amount) if counts[i] < largest] or [i for i in range(1, amount) if counts[i] < limit]
        pool, remaining = sum([weights[i] for i in free]), spare
        for i in free:
            more = min(limit - counts[i], max(1, remaining * weights[i] // pool), spare)
            counts[i] = counts[i] + more
            spare = spare - more
    return np.array(counts)


def scatter_about(own_key, shape, scale, limit, split=(), kind=jnp.bfloat16):
    result = jax.random.normal(own_key, shape, jnp.float32) * scale
    if len(split) > 0:
        result = block_scale(own_key, shape, split, -0.22, 0.18) * result
    return jnp.clip(result, min=-limit, max=limit).astype(kind)


def setup_inputs(seed: int = 0) -> dict:
    key_of = jax.random.split(jax.random.key(seed), 18)
    hidden_in = scatter_about(key_of[0], (TOKENS, D), 1.0, 6.0, ((0, 32),))
    seq_lengths = draw_seq_lengths(jax.random.fold_in(key_of[17], 71), 0)
    seq_offsets = draw_seq_offsets(jax.random.fold_in(key_of[17], 71), 0)
    routes_keys = jax.random.split(jax.random.fold_in(key_of[3], 1), TOKENS // TOK_DEV)
    routes_turns = jax.random.permutation(jax.random.fold_in(key_of[3], 3), TOKENS // TOK_DEV)
    routes = jax.vmap(lambda own, number: routed_block(jax.random.fold_in(key_of[3], 2), own, number, TOK_DEV, EXPERTS, TOP, CAP, 1))(routes_keys, routes_turns).reshape((TOKENS, TOP))
    attn_gain = jnp.clip(1.0 + 0.1 * jax.random.normal(key_of[4], (D,), jnp.float32), 0.5, 1.5)
    w_query = scatter_about(key_of[5], (D, H * HD), D ** -0.5, 0.125, ((0, 8), (1, 4)), jnp.float32)
    w_key = scatter_about(key_of[6], (D, H * HD), D ** -0.5, 0.125, ((0, 8), (1, 4)), jnp.float32)
    w_value = scatter_about(key_of[7], (D, H * HD), D ** -0.5, 0.125, ((0, 8), (1, 4)), jnp.float32)
    query_gain = jnp.clip(1.0 + 0.1 * jax.random.normal(key_of[8], (HD,), jnp.float32), 0.5, 1.5)
    key_gain = jnp.clip(1.0 + 0.1 * jax.random.normal(key_of[9], (HD,), jnp.float32), 0.5, 1.5)
    w_output = scatter_about(key_of[10], (H * HD, D), (4 * H * HD // GROUP) ** -0.5, 2.0, ((0, 4), (1, 8)), jnp.float32)
    ffn_gain = jnp.clip(1.0 + 0.1 * jax.random.normal(key_of[11], (D,), jnp.float32), 0.5, 1.5)
    router = scatter_about(key_of[12], (D, EXPERTS), (4 * D) ** -0.5, 0.0625, ((0, 8),), jnp.float32)
    w_gate = scatter_about(key_of[13], (EXPERTS, D, FF), D ** -0.5, 0.125, ((0, 8), (2, 4)), jnp.float32)
    w_up = scatter_about(key_of[14], (EXPERTS, D, FF), D ** -0.5, 0.125, ((0, 8), (2, 4)), jnp.float32)
    w_down = scatter_about(key_of[15], (EXPERTS, FF, D), (0.7 * EXPERTS * FF ** -0.5), 2.0, ((0, 8), (1, 4)), jnp.float32)
    cotangent = scatter_about(key_of[16], (TOKENS, D), 1.0, 6.0, ((0, 32),), jnp.float32)
    return {"hidden_in": hidden_in, "seq_lengths": seq_lengths, "seq_offsets": seq_offsets, "routes": routes, "attn_gain": attn_gain, "w_query": w_query, "w_key": w_key, "w_value": w_value, "query_gain": query_gain, "key_gain": key_gain, "w_output": w_output, "ffn_gain": ffn_gain, "router": router, "w_gate": w_gate, "w_up": w_up, "w_down": w_down, "cotangent": cotangent}


@jax.custom_vjp
def low(v):
    return lax.optimization_barrier(v.astype(jnp.bfloat16)).astype(jnp.float32)

@jax.custom_vjp
def low_back(v):
    return v

def low_keep(v):
    return (low(v), None)

def low_pass(kept, grad):
    return (grad,)

def back_keep(v):
    return (v, None)

def back_low(kept, grad):
    return (low(grad),)
low.defvjp(low_keep, low_pass)
low_back.defvjp(back_keep, back_low)
NORM_EPSILON = 1e-06
ROPE_THETA = 10000.0

def precise(left, right):
    return jnp.dot(left, right, precision=lax.Precision.HIGHEST)

def rms_norm(values, gain_vec):
    return values * lax.rsqrt(lax.optimization_barrier(jnp.mean(values * values, axis=-1, keepdims=True)) + NORM_EPSILON) * gain_vec

def rotary_tables(positions, width):
    half_width = width // 2
    frequency = ROPE_THETA ** (-(jnp.arange(half_width, dtype=jnp.float32) * 2.0 / width))
    angles = positions.astype(jnp.float32)[:, None] * frequency[None, :]
    angles = jnp.concatenate([angles, angles], axis=1)
    return (jnp.cos(angles), jnp.sin(angles))

def rotary(values, cos_table, sin_table):
    half_width = values.shape[-1] // 2
    rotated = jnp.concatenate([-values[..., half_width:], values[..., :half_width]], axis=-1)
    return values * cos_table[:, None, :] + rotated * sin_table[:, None, :]

def attend_group(normed, row_start, row_length, query_w, key_w, value_w, gain_query, gain_key):
    seq_rows = normed.shape[0]
    query_pre = low_back(precise(normed, query_w)).reshape(seq_rows, H, HD)
    key_pre = low_back(precise(normed, key_w)).reshape(seq_rows, H, HD)
    value_low = low(low_back(precise(normed, value_w))).reshape(seq_rows, H, HD)
    row_place = jnp.arange(seq_rows, dtype=jnp.int32)
    cos_table, sin_table = rotary_tables(row_place - row_start, HD)
    query_low = low(rotary(rms_norm(query_pre, gain_query), cos_table, sin_table))
    key_low = low(rotary(rms_norm(key_pre, gain_key), cos_table, sin_table))
    key_valid = (row_place >= row_start) & (row_place < row_start + row_length)
    scores = jnp.einsum('qhd,khd->hqk', query_low, key_low, precision=lax.Precision.HIGHEST)
    scores = low_back(scores * HD ** (-0.5))
    scores = jnp.where(key_valid[None, None, :], scores, -1e+30)
    attn_prob = low(jax.nn.softmax(scores, axis=-1))
    mixed_out = jnp.einsum('hqk,khd->qhd', attn_prob, value_low, precision=lax.Precision.HIGHEST)
    return low(low_back(mixed_out)).reshape(seq_rows, H * HD)

def expert(rows_in, gate_w, up_w, down_w):
    gate_val = low_back(precise(rows_in, gate_w))
    up_val = low_back(precise(rows_in, up_w))
    hidden = low(jax.nn.silu(gate_val) * up_val)
    return low_back(low(precise(hidden, down_w)))

def expert_item(items):
    return expert(items[0], items[1], items[2], items[3])

def reference(hidden_in, seq_lengths, seq_offsets, routes, attn_gain, w_query, w_key, w_value, query_gain, key_gain, w_output, ffn_gain, router, w_gate, w_up, w_down, cotangent):
    group_rows = TOK_DEV * N_TP
    blocks = N_FSDP * N_TP
    assigned_count = TOK_DEV * TOP
    row_place = jnp.arange(group_rows, dtype=jnp.int32)
    row_valid = (row_place[None, :] >= seq_offsets[:, None]) & (row_place[None, :] < (seq_offsets + seq_lengths)[:, None])
    row_keep = row_valid.reshape(TOKENS, 1).astype(jnp.float32)
    assigned = routes.reshape(blocks, assigned_count)
    one_hot = (assigned[:, :, None] == jnp.arange(EXPERTS, dtype=jnp.int32)[None, None, :]).astype(jnp.int32)
    slot_rank = lax.optimization_barrier(jnp.sum((jnp.cumsum(one_hot, axis=1) - 1) * one_hot, axis=2)).astype(jnp.int32)
    block_ids = jnp.arange(blocks, dtype=jnp.int32)[:, None]
    token_ids = (block_ids * TOK_DEV + jnp.arange(assigned_count, dtype=jnp.int32)[None, :] // TOP).astype(jnp.int32)
    slot_place = (assigned * (blocks * CAP) + block_ids * CAP + slot_rank).astype(jnp.int32)
    source_row = jnp.full((EXPERTS * blocks * CAP,), TOKENS, jnp.int32).at[slot_place.reshape(-1)].set(token_ids.reshape(-1))
    slot_place = slot_place.reshape(TOKENS, TOP)

    def forward(source, gain_attn, query_w, key_w, value_w, gain_query, gain_key, output_w, gain_ffn, router_w, gate_w, up_w, down_w):
        gain_attn = low(gain_attn)
        query_w = low(query_w)
        key_w = low(key_w)
        value_w = low(value_w)
        gain_query = low(gain_query)
        gain_key = low(gain_key)
        output_w = low(output_w)
        gain_ffn = low(gain_ffn)
        router_w = low(router_w)
        gate_w = low(gate_w)
        up_w = low(up_w)
        down_w = low(down_w)
        normed = low(rms_norm(source, gain_attn))

        def group_item(items):
            return attend_group(items[0], items[1], items[2], query_w, key_w, value_w, gain_query, gain_key)
        mixed_out = lax.map(jax.checkpoint(group_item), (normed.reshape(N_FSDP, group_rows, D), seq_offsets, seq_lengths))
        attn_out = low_back(precise(mixed_out.reshape(TOKENS, H * HD), output_w))
        residual = source + row_keep * attn_out
        ffn_normed = low(rms_norm(residual, gain_ffn))
        logits = low_back(precise(ffn_normed, router_w))
        gate_weights = jnp.take_along_axis(jax.nn.softmax(logits, axis=-1), routes, axis=1)
        padded = jnp.concatenate([ffn_normed, jnp.zeros((1, D), jnp.float32)], axis=0)
        sent_rows = low_back(padded[source_row]).reshape(EXPERTS, blocks * CAP, D)
        expert_out = lax.map(jax.checkpoint(expert_item), (sent_rows, gate_w, up_w, down_w)).reshape(EXPERTS * blocks * CAP, D)
        mixture = jnp.zeros((TOKENS, D), jnp.float32)
        for route_slot in range(TOP):
            mixture = mixture + gate_weights[:, route_slot:route_slot + 1] * expert_out[slot_place[:, route_slot]]
        return residual + row_keep * mixture
    primals = (hidden_in.astype(jnp.float32), attn_gain, w_query, w_key, w_value, query_gain, key_gain, w_output, ffn_gain, router, w_gate, w_up, w_down)
    block_out, pullback = jax.vjp(forward, *primals)
    gradients = pullback(cotangent)
    return (block_out.astype(jnp.bfloat16), gradients[0], gradients[1], gradients[2], gradients[3], gradients[4], gradients[5], gradients[6], gradients[7], gradients[8], gradients[9], gradients[10], gradients[11], gradients[12])
```

```python
import functools

import jax
import jax.numpy as jnp
from jax import lax
from jax.sharding import PartitionSpec as P

HD = 128


NORM_EPSILON = 1e-06
ROPE_THETA = 10000.0


def rms_norm(values, gain_vec):
    return (
        values
        * lax.rsqrt(jnp.mean(values * values, axis=-1, keepdims=True) + NORM_EPSILON)
        * gain_vec
    )


def rotary_tables(positions, width):
    half_width = width // 2
    frequency = ROPE_THETA ** (-(jnp.arange(half_width, dtype=jnp.float32) * 2.0 / width))
    angles = positions.astype(jnp.float32)[:, None] * frequency[None, :]
    angles = jnp.concatenate([angles, angles], axis=1)
    return (jnp.cos(angles), jnp.sin(angles))


def head_prepare(pre_values, gain_vec, cos_table, sin_table):
    seq_rows = pre_values.shape[0]
    shaped = pre_values.reshape(seq_rows, -1, gain_vec.shape[0])
    normed = rms_norm(shaped, gain_vec)
    half_width = gain_vec.shape[0] // 2
    rotated = jnp.concatenate([-normed[..., half_width:], normed[..., :half_width]], axis=-1)
    turned = normed * cos_table[:, None, :] + rotated * sin_table[:, None, :]
    return turned.reshape(pre_values.shape)


def swiglu(gate_val, up_val):
    return jax.nn.silu(gate_val) * up_val


def gate_pick(logits, one_hot):
    return jnp.sum(jax.nn.softmax(logits, axis=-1)[:, None, :] * one_hot, axis=-1)


def whole_group(values):
    return lax.all_gather(values, "tp", axis=0, tiled=True)


def head_sum(term_fn, rows_local):
    return lax.psum_scatter(
        term_fn(jnp.int32(0), lax.axis_size("tp") * rows_local).astype(jnp.bfloat16),
        "tp",
        scatter_dimension=0,
        tiled=True,
    ).astype(jnp.float32)


def to_experts(buffer):
    return lax.all_to_all(buffer, "fsdp", split_axis=0, concat_axis=0, tiled=True)


def from_experts(buffer):
    return lax.all_to_all(buffer, "fsdp", split_axis=0, concat_axis=0, tiled=True)


def per_device_routed(
    hidden_in,
    seq_lengths,
    seq_offsets,
    routes,
    attn_gain,
    w_query,
    w_key,
    w_value,
    query_gain,
    key_gain,
    w_output,
    ffn_gain,
    router,
    w_gate,
    w_up,
    w_down,
    cotangent,
):
    tp_size = lax.axis_size("tp")
    rows_local = hidden_in.shape[0]
    model_width = hidden_in.shape[1]
    group_rows = rows_local * tp_size
    top_count = routes.shape[1]
    experts = router.shape[1]
    expert_local = w_gate.shape[0]
    fsdp_count = experts // expert_local
    capacity = 9 * rows_local * top_count // (8 * experts)
    heads_local = w_output.shape[0] // HD
    block_rows = min(512, group_rows)
    block_count = group_rows // block_rows
    score_scale = HD ** (-0.5)
    row_first = lax.axis_index("tp") * rows_local
    seq_start = seq_offsets[0]
    seq_end = seq_start + seq_lengths[0]
    group_place = jnp.arange(group_rows, dtype=jnp.int32)
    key_valid = (group_place >= seq_start) & (group_place < seq_end)
    local_place = row_first + jnp.arange(rows_local, dtype=jnp.int32)
    row_keep = ((local_place >= seq_start) & (local_place < seq_end)).astype(jnp.float32)[:, None]
    cos_table, sin_table = rotary_tables(group_place - seq_start, HD)
    (
        gain_attn,
        gain_query,
        gain_key,
        gain_ffn,
        router_full,
        query_full,
        key_full,
        value_full,
        output_full,
    ) = (
        lax.all_gather(attn_gain.astype(jnp.bfloat16), "fsdp", axis=0, tiled=True),
        lax.all_gather(query_gain.astype(jnp.bfloat16), "fsdp", axis=0, tiled=True),
        lax.all_gather(key_gain.astype(jnp.bfloat16), "fsdp", axis=0, tiled=True),
        lax.all_gather(ffn_gain.astype(jnp.bfloat16), "fsdp", axis=0, tiled=True),
        lax.all_gather(router.astype(jnp.bfloat16), "fsdp", axis=0, tiled=True),
        lax.all_gather(w_query.astype(jnp.bfloat16), "fsdp", axis=0, tiled=True),
        lax.all_gather(w_key.astype(jnp.bfloat16), "fsdp", axis=0, tiled=True),
        lax.all_gather(w_value.astype(jnp.bfloat16), "fsdp", axis=0, tiled=True),
        lax.all_gather(w_output.astype(jnp.bfloat16), "fsdp", axis=1, tiled=True),
    )
    residual_in = hidden_in.astype(jnp.float32)
    attn_gain_f = gain_attn.astype(jnp.float32)
    normed = rms_norm(residual_in, attn_gain_f).astype(jnp.bfloat16)
    group_normed = whole_group(normed)
    query_pre = jnp.dot(group_normed, query_full, preferred_element_type=jnp.float32)
    key_pre = jnp.dot(group_normed, key_full, preferred_element_type=jnp.float32)
    value_low = jnp.dot(group_normed, value_full, preferred_element_type=jnp.float32).astype(
        jnp.bfloat16
    )
    query_gain_f = gain_query.astype(jnp.float32)
    key_gain_f = gain_key.astype(jnp.float32)
    query_low = head_prepare(query_pre, query_gain_f, cos_table, sin_table).astype(jnp.bfloat16)
    key_low = head_prepare(key_pre, key_gain_f, cos_table, sin_table).astype(jnp.bfloat16)
    key_heads = key_low.reshape(group_rows, heads_local, HD)
    value_heads = value_low.reshape(group_rows, heads_local, HD)
    query_blocks = query_low.reshape(block_count, block_rows, heads_local, HD)

    def forward_block(query_block):
        scores = (
            jnp.einsum("qhd,khd->hqk", query_block, key_heads, preferred_element_type=jnp.float32)
            * score_scale
        )
        scores = jnp.where(key_valid[None, None, :], scores, -1e30)
        row_max = jnp.max(scores, axis=-1, keepdims=True)
        exp_scores = jnp.exp(scores - row_max)
        row_total = jnp.sum(exp_scores, axis=-1, keepdims=True)
        attn_prob = (exp_scores / row_total).astype(jnp.bfloat16)
        mixed_block = jnp.einsum(
            "hqk,khd->qhd", attn_prob, value_heads, preferred_element_type=jnp.float32
        )
        return (mixed_block.astype(jnp.bfloat16), (row_max + jnp.log(row_total))[..., 0])

    mixed_blocks, log_totals = lax.map(forward_block, query_blocks)
    mixed_out = mixed_blocks.reshape(group_rows, heads_local * HD)

    def attn_term(row_start, row_count):
        return jnp.dot(mixed_out, output_full, preferred_element_type=jnp.float32)

    attn_out = head_sum(attn_term, rows_local)
    residual = residual_in + row_keep * attn_out
    ffn_gain_f = gain_ffn.astype(jnp.float32)
    ffn_normed = rms_norm(residual, ffn_gain_f).astype(jnp.bfloat16)
    logits = jnp.dot(ffn_normed, router_full, preferred_element_type=jnp.float32)
    one_hot_routes = (
        routes[:, :, None] == jnp.arange(experts, dtype=jnp.int32)[None, None, :]
    ).astype(jnp.float32)
    gate_weights = gate_pick(logits, one_hot_routes)
    expert_of = routes.reshape(-1)
    assign_count = rows_local * top_count
    assign_hot = (expert_of[:, None] == jnp.arange(experts, dtype=jnp.int32)[None, :]).astype(
        jnp.int32
    )
    slot_rank = jnp.sum((jnp.cumsum(assign_hot, axis=0) - 1) * assign_hot, axis=1)
    slot_place = expert_of * capacity + slot_rank
    slot_owner = (
        jnp.full((experts * capacity,), assign_count, jnp.int32)
        .at[slot_place]
        .set(jnp.arange(assign_count, dtype=jnp.int32))
    )
    padded = jnp.concatenate([ffn_normed, jnp.zeros((1, model_width), jnp.bfloat16)], axis=0)
    sent_rows = padded[slot_owner // top_count].reshape(
        fsdp_count, expert_local, capacity, model_width
    )
    arrived = to_experts(sent_rows)
    gate_local = w_gate.astype(jnp.bfloat16)
    up_local = w_up.astype(jnp.bfloat16)
    down_local = w_down.astype(jnp.bfloat16)
    gate_full, up_full, down_full = (
        lax.all_gather(gate_local, "tp", axis=2, tiled=True),
        lax.all_gather(up_local, "tp", axis=2, tiled=True),
        lax.all_gather(down_local, "tp", axis=1, tiled=True),
    )
    gate_val = jnp.einsum("secd,edf->secf", arrived, gate_full, preferred_element_type=jnp.float32)
    up_val = jnp.einsum("secd,edf->secf", arrived, up_full, preferred_element_type=jnp.float32)
    hidden = swiglu(gate_val, up_val).astype(jnp.bfloat16)
    expert_out = jnp.einsum(
        "secf,efd->secd", hidden, down_full, preferred_element_type=jnp.float32
    ).astype(jnp.bfloat16)
    returned = from_experts(expert_out).reshape(experts * capacity, model_width)
    out_rows = returned[slot_place].reshape(rows_local, top_count, model_width).astype(jnp.float32)
    mixture = jnp.sum(gate_weights[:, :, None] * out_rows, axis=1)
    block_out = (residual + row_keep * mixture).astype(jnp.bfloat16)
    grad_mixture = row_keep * cotangent
    grad_gates = jnp.sum(grad_mixture[:, None, :] * out_rows, axis=-1)
    grad_slots = (
        (gate_weights[:, :, None] * grad_mixture[:, None, :])
        .astype(jnp.bfloat16)
        .reshape(assign_count, model_width)
    )
    grad_padded = jnp.concatenate([grad_slots, jnp.zeros((1, model_width), jnp.bfloat16)], axis=0)
    grad_sent = grad_padded[slot_owner].reshape(fsdp_count, expert_local, capacity, model_width)
    grad_arrived = to_experts(grad_sent)
    grad_hidden = jnp.einsum(
        "secd,efd->secf", grad_arrived, down_full, preferred_element_type=jnp.float32
    )
    full_down_grad = jnp.einsum(
        "secf,secd->efd", hidden, grad_arrived, preferred_element_type=jnp.float32
    )
    grad_gate_val, grad_up_val = jax.vjp(swiglu, gate_val, up_val)[1](grad_hidden)
    grad_gate_low = grad_gate_val.astype(jnp.bfloat16)
    grad_up_low = grad_up_val.astype(jnp.bfloat16)
    full_gate_grad = jnp.einsum(
        "secd,secf->edf", arrived, grad_gate_low, preferred_element_type=jnp.float32
    )
    full_up_grad = jnp.einsum(
        "secd,secf->edf", arrived, grad_up_low, preferred_element_type=jnp.float32
    )
    grad_w_gate, grad_w_up, grad_w_down = (
        lax.psum_scatter(
            full_gate_grad.astype(jnp.bfloat16), "tp", scatter_dimension=2, tiled=True
        ).astype(jnp.float32),
        lax.psum_scatter(
            full_up_grad.astype(jnp.bfloat16), "tp", scatter_dimension=2, tiled=True
        ).astype(jnp.float32),
        lax.psum_scatter(
            full_down_grad.astype(jnp.bfloat16), "tp", scatter_dimension=1, tiled=True
        ).astype(jnp.float32),
    )
    grad_back = (
        jnp.einsum("secf,edf->secd", grad_gate_low, gate_full, preferred_element_type=jnp.float32)
        + jnp.einsum("secf,edf->secd", grad_up_low, up_full, preferred_element_type=jnp.float32)
    ).astype(jnp.bfloat16)
    grad_returned = from_experts(grad_back).reshape(experts * capacity, model_width)
    grad_from_slots = jnp.sum(
        grad_returned[slot_place].reshape(rows_local, top_count, model_width).astype(jnp.float32),
        axis=1,
    )
    grad_logits = jax.vjp(functools.partial(gate_pick, one_hot=one_hot_routes), logits)[1](
        grad_gates
    )[0].astype(jnp.bfloat16)
    grad_router_local = jnp.einsum(
        "td,te->de", ffn_normed, grad_logits, preferred_element_type=jnp.float32
    )
    grad_ffn_normed = grad_from_slots + jnp.einsum(
        "te,de->td", grad_logits, router_full, preferred_element_type=jnp.float32
    )
    grad_residual_part, grad_ffn_gain_local = jax.vjp(rms_norm, residual, ffn_gain_f)[1](
        grad_ffn_normed
    )
    grad_residual = cotangent + grad_residual_part
    grad_attn = (row_keep * grad_residual).astype(jnp.bfloat16)
    grad_attn_all = whole_group(grad_attn)
    grad_mixed = jnp.einsum(
        "gd,hd->gh", grad_attn_all, output_full, preferred_element_type=jnp.float32
    ).astype(jnp.bfloat16)
    grad_output_local = jnp.einsum(
        "gh,gd->hd", mixed_out, grad_attn_all, preferred_element_type=jnp.float32
    )
    grad_mixed_blocks = grad_mixed.reshape(block_count, block_rows, heads_local, HD)

    def backward_block(totals, block_in):
        key_total, value_total = totals
        query_block, grad_block, log_block = block_in
        scores = (
            jnp.einsum("qhd,khd->hqk", query_block, key_heads, preferred_element_type=jnp.float32)
            * score_scale
        )
        scores = jnp.where(key_valid[None, None, :], scores, -1e30)
        attn_prob = jnp.exp(scores - log_block[..., None])
        prob_low = attn_prob.astype(jnp.bfloat16)
        value_total = value_total + jnp.einsum(
            "hqk,qhd->khd", prob_low, grad_block, preferred_element_type=jnp.float32
        )
        grad_prob = jnp.einsum(
            "qhd,khd->hqk", grad_block, value_heads, preferred_element_type=jnp.float32
        )
        row_delta = jnp.sum(attn_prob * grad_prob, axis=-1, keepdims=True)
        grad_scores = (attn_prob * (grad_prob - row_delta)).astype(jnp.bfloat16)
        grad_query_block = (
            jnp.einsum("hqk,khd->qhd", grad_scores, key_heads, preferred_element_type=jnp.float32)
            * score_scale
        )
        key_total = (
            key_total
            + jnp.einsum(
                "hqk,qhd->khd", grad_scores, query_block, preferred_element_type=jnp.float32
            )
            * score_scale
        )
        return ((key_total, value_total), grad_query_block)

    zero_heads = jnp.zeros((group_rows, heads_local, HD), jnp.float32)
    (grad_key, grad_value), grad_query_blocks = lax.scan(
        backward_block, (zero_heads, zero_heads), (query_blocks, grad_mixed_blocks, log_totals)
    )
    grad_query = grad_query_blocks.reshape(group_rows, heads_local * HD)
    prepare_fn = functools.partial(head_prepare, cos_table=cos_table, sin_table=sin_table)
    grad_query_pre, grad_query_gain_local = jax.vjp(prepare_fn, query_pre, query_gain_f)[1](
        grad_query
    )
    grad_key_pre, grad_key_gain_local = jax.vjp(prepare_fn, key_pre, key_gain_f)[1](
        grad_key.reshape(group_rows, heads_local * HD)
    )
    grad_query_low = grad_query_pre.astype(jnp.bfloat16)
    grad_key_low = grad_key_pre.astype(jnp.bfloat16)
    grad_value_low = grad_value.reshape(group_rows, heads_local * HD).astype(jnp.bfloat16)
    grad_query_w = jnp.einsum(
        "gd,gh->dh", group_normed, grad_query_low, preferred_element_type=jnp.float32
    )
    grad_key_w = jnp.einsum(
        "gd,gh->dh", group_normed, grad_key_low, preferred_element_type=jnp.float32
    )
    grad_value_w = jnp.einsum(
        "gd,gh->dh", group_normed, grad_value_low, preferred_element_type=jnp.float32
    )

    def input_term(row_start, row_count):
        summed = jnp.einsum(
            "gh,dh->gd", grad_query_low, query_full, preferred_element_type=jnp.float32
        )
        summed = summed + jnp.einsum(
            "gh,dh->gd", grad_key_low, key_full, preferred_element_type=jnp.float32
        )
        return summed + jnp.einsum(
            "gh,dh->gd", grad_value_low, value_full, preferred_element_type=jnp.float32
        )

    grad_normed = head_sum(input_term, rows_local)
    grad_input_part, grad_attn_gain_local = jax.vjp(rms_norm, residual_in, attn_gain_f)[1](
        grad_normed
    )
    grad_input = grad_residual + grad_input_part
    grad_w_query, grad_w_key, grad_w_value, grad_w_output = (
        lax.psum_scatter(
            grad_query_w.astype(jnp.bfloat16), "fsdp", scatter_dimension=0, tiled=True
        ).astype(jnp.float32),
        lax.psum_scatter(
            grad_key_w.astype(jnp.bfloat16), "fsdp", scatter_dimension=0, tiled=True
        ).astype(jnp.float32),
        lax.psum_scatter(
            grad_value_w.astype(jnp.bfloat16), "fsdp", scatter_dimension=0, tiled=True
        ).astype(jnp.float32),
        lax.psum_scatter(
            grad_output_local.astype(jnp.bfloat16), "fsdp", scatter_dimension=1, tiled=True
        ).astype(jnp.float32),
    )
    grad_attn_gain, grad_query_gain, grad_key_gain, grad_ffn_gain, grad_router = (
        lax.psum_scatter(grad_attn_gain_local, ("fsdp", "tp"), scatter_dimension=0, tiled=True),
        lax.psum_scatter(grad_query_gain_local, ("fsdp", "tp"), scatter_dimension=0, tiled=True),
        lax.psum_scatter(grad_key_gain_local, ("fsdp", "tp"), scatter_dimension=0, tiled=True),
        lax.psum_scatter(grad_ffn_gain_local, ("fsdp", "tp"), scatter_dimension=0, tiled=True),
        lax.psum_scatter(grad_router_local, ("fsdp", "tp"), scatter_dimension=0, tiled=True),
    )
    return (
        block_out,
        grad_input,
        grad_attn_gain,
        grad_w_query,
        grad_w_key,
        grad_w_value,
        grad_query_gain,
        grad_key_gain,
        grad_w_output,
        grad_ffn_gain,
        grad_router,
        grad_w_gate,
        grad_w_up,
        grad_w_down,
    )


def pair_swap(values, distance):
    count = lax.axis_size("tp")
    return lax.ppermute(values, "tp", [(i, i ^ distance) for i in range(count)])


def shift_tp(values, step, first, last):
    return lax.ppermute(values, "tp", [(i, i + step) for i in range(first, last + 1)])


def line_gather(values):
    right, left, from_left, from_right = (values, values, [], [])
    for step in range(3):
        right = shift_tp(right, 1, step, 2)
        left = shift_tp(left, -1, 1, 3 - step)
        from_left.append(right)
        from_right.append(left)
    place = lax.axis_index("tp")
    blocks = [values]
    for offset in range(1, 4):
        blocks.append(jnp.where(place >= offset, from_left[offset - 1], from_right[3 - offset]))
    return jnp.concatenate(blocks, axis=0)


def line_scatter(blocks):
    right, left = (None, None)
    for step in range(3):
        to_right, to_left = (blocks[step + 1], blocks[3 - step])
        if step > 0:
            to_right = to_right.astype(jnp.float32) + right.astype(jnp.float32)
            to_left = to_left.astype(jnp.float32) + left.astype(jnp.float32)
        right = shift_tp(to_right.astype(jnp.bfloat16), 1, 0, step)
        left = shift_tp(to_left.astype(jnp.bfloat16), -1, 3 - step, 3)
    return (
        blocks[0].astype(jnp.float32) + right.astype(jnp.float32) + left.astype(jnp.float32)
    )


def gather_plane(values):
    return lax.all_gather(values, "fsdp", axis=0, tiled=True)


def scatter_plane(values):
    return lax.psum_scatter(values, "fsdp", scatter_dimension=0, tiled=True)


def matmul(left, right, left_dim, right_dim):
    return lax.dot_general(
        left,
        right,
        (((left_dim,), (right_dim,)), ((), ())),
        preferred_element_type=jnp.float32,
    )


def per_device_dense(
    hidden_in,
    seq_lengths,
    seq_offsets,
    routes,
    attn_gain,
    w_query,
    w_key,
    w_value,
    query_gain,
    key_gain,
    w_output,
    ffn_gain,
    router,
    w_gate,
    w_up,
    w_down,
    cotangent,
):
    low = jnp.bfloat16
    full = jnp.float32
    tp_size = lax.axis_size("tp")
    fsdp_size = lax.axis_size("fsdp")
    tp_place = lax.axis_index("tp")
    fsdp_place = lax.axis_index("fsdp")
    rows, width = hidden_in.shape
    group_rows = rows * tp_size
    experts = router.shape[1]
    expert_local = w_gate.shape[0]
    quarter = w_gate.shape[2]
    shard = w_query.shape[0]
    head_width = w_query.shape[1]
    heads = head_width // HD
    block_rows = min(512, group_rows)
    block_count = group_rows // block_rows
    score_scale = HD ** (-0.5)
    seq_start = seq_offsets[0]
    seq_end = seq_start + seq_lengths[0]

    group_hidden = line_gather(hidden_in)
    order = jnp.mod(tp_place - jnp.arange(tp_size, dtype=jnp.int32), tp_size)
    group_place = (
        order[:, None] * rows + jnp.arange(rows, dtype=jnp.int32)[None, :]
    ).reshape(group_rows)
    key_valid = (group_place >= seq_start) & (group_place < seq_end)
    row_keep = key_valid[:rows].astype(full)[:, None]
    cos_table, sin_table = rotary_tables(group_place - seq_start, HD)

    small = jnp.zeros((shard, 128), low)
    small = small.at[:, :experts].set(router.astype(low))
    small = small.at[:, experts].set(attn_gain.astype(low))
    small = small.at[:, experts + 1].set(ffn_gain.astype(low))
    small = small.at[: query_gain.shape[0], experts + 2].set(query_gain.astype(low))
    small = small.at[: key_gain.shape[0], experts + 3].set(key_gain.astype(low))
    packed = jnp.concatenate(
        [
            w_query.astype(low),
            w_key.astype(low),
            w_value.astype(low),
            w_output.astype(low).T,
            small,
        ],
        axis=1,
    )
    packed_full = gather_plane(packed)
    w_qkv = packed_full[:, : 3 * head_width]
    w_out_t = packed_full[:, 3 * head_width : 4 * head_width]
    small_full = packed_full[:, 4 * head_width :]
    small_t = small_full.T
    router_full = small_full[:, :experts]
    attn_gain_f = small_t[experts].astype(full)
    ffn_gain_f = small_t[experts + 1].astype(full)
    gain_piece = query_gain.shape[0]
    query_gain_f = small_t[experts + 2].reshape(fsdp_size, shard)[:, :gain_piece].reshape(-1)
    key_gain_f = small_t[experts + 3].reshape(fsdp_size, shard)[:, :gain_piece].reshape(-1)
    query_gain_f = query_gain_f.astype(full)
    key_gain_f = key_gain_f.astype(full)

    expert_ids = jnp.arange(experts, dtype=jnp.int32)
    own_mask = jnp.sum(
        (routes[:, :, None] == expert_ids[None, None, :]).astype(full), axis=1
    ) * row_keep
    mask_low = own_mask.astype(low)
    grad_low = cotangent.astype(low)
    mask_parts = [gather_plane(mask_low), gather_plane(pair_swap(mask_low, 2))]
    grad_parts = [gather_plane(grad_low), gather_plane(pair_swap(grad_low, 2))]

    gate_own = jnp.concatenate([w_gate[e] for e in range(expert_local)], axis=1).astype(low)
    up_own = jnp.concatenate([w_up[e] for e in range(expert_local)], axis=1).astype(low)
    down_own = w_down.reshape(expert_local * quarter, width).astype(low)
    gate_all = jnp.concatenate([gate_own, pair_swap(gate_own, 1)], axis=1)
    up_all = jnp.concatenate([up_own, pair_swap(up_own, 1)], axis=1)
    down_all = jnp.concatenate([down_own, pair_swap(down_own, 1)], axis=0)

    group_full = group_hidden.astype(full)
    row_scale = lax.rsqrt(jnp.mean(group_full * group_full, axis=-1, keepdims=True) + NORM_EPSILON)
    group_normed = (group_full * row_scale * attn_gain_f).astype(low)
    qkv_pre = matmul(group_normed, w_qkv, 1, 0)
    query_pre = qkv_pre[:, :head_width]
    key_pre = qkv_pre[:, head_width : 2 * head_width]
    value_low = qkv_pre[:, 2 * head_width :].astype(low)
    query_low = head_prepare(query_pre, query_gain_f, cos_table, sin_table).astype(low)
    key_low = head_prepare(key_pre, key_gain_f, cos_table, sin_table).astype(low)
    key_heads = key_low.reshape(group_rows, heads, HD)
    value_heads = value_low.reshape(group_rows, heads, HD)
    query_blocks = query_low.reshape(block_count, block_rows, heads, HD)

    def forward_block(query_block):
        scores = (
            jnp.einsum("qhd,khd->hqk", query_block, key_heads, preferred_element_type=full)
            * score_scale
        )
        scores = jnp.where(key_valid[None, None, :], scores, -1e30)
        row_max = jnp.max(scores, axis=-1, keepdims=True)
        exp_scores = jnp.exp(scores - row_max)
        row_total = jnp.sum(exp_scores, axis=-1, keepdims=True)
        attn_prob = (exp_scores / row_total).astype(low)
        mixed_block = jnp.einsum(
            "hqk,khd->qhd", attn_prob, value_heads, preferred_element_type=full
        )
        return (mixed_block.astype(low), (row_max + jnp.log(row_total))[..., 0])

    mixed_blocks, log_totals = lax.map(forward_block, query_blocks)
    mixed_out = mixed_blocks.reshape(group_rows, heads * HD)
    attn_term = matmul(mixed_out, w_out_t, 1, 1).astype(low)
    attn_out = line_scatter([attn_term[k * rows : (k + 1) * rows] for k in range(tp_size)])
    hidden_full = hidden_in.astype(full)
    residual = hidden_full + row_keep * attn_out
    ffn_scale = lax.rsqrt(jnp.mean(residual * residual, axis=-1, keepdims=True) + NORM_EPSILON)
    ffn_normed = (residual * ffn_scale * ffn_gain_f).astype(low)
    row_parts = [gather_plane(ffn_normed), gather_plane(pair_swap(ffn_normed, 2))]
    probs = jax.nn.softmax(matmul(ffn_normed, router_full, 1, 0), axis=-1)

    saved = []
    gate_grads = []
    for part in range(2):
        part_rows, part_grad, part_mask = (row_parts[part], grad_parts[part], mask_parts[part])
        part_gate = jax.nn.softmax(matmul(part_rows, router_full, 1, 0), axis=-1) * part_mask
        chosen = [
            (expert_ids == fsdp_place * expert_local + e).astype(full)[None, :]
            for e in range(expert_local)
        ]
        gates = [jnp.sum(part_gate * pick, axis=1, keepdims=True) for pick in chosen]
        masks = [jnp.sum(part_mask.astype(full) * pick, axis=1) for pick in chosen]
        spread = jnp.concatenate(
            [
                jnp.broadcast_to(gates[e], (gates[e].shape[0], quarter))
                for _ in range(2)
                for e in range(expert_local)
            ],
            axis=1,
        )
        gate_val = matmul(part_rows, gate_all, 1, 0)
        up_val = matmul(part_rows, up_all, 1, 0)
        grad_hidden = matmul(part_grad, down_all, 1, 1)
        sigma = jax.nn.sigmoid(gate_val)
        silu = gate_val * sigma
        hidden = (silu * up_val).astype(low)
        product = hidden.astype(full) * grad_hidden
        gate_grads.append(
            jnp.stack(
                [
                    jnp.sum(
                        product[:, e * quarter : (e + 1) * quarter]
                        + product[
                            :, (expert_local + e) * quarter : (expert_local + e + 1) * quarter
                        ],
                        axis=1,
                    )
                    * masks[e]
                    for e in range(expert_local)
                ],
                axis=0,
            )
        )
        scaled = spread * grad_hidden
        grad_gate_low = (scaled * up_val * (sigma * (1.0 + gate_val * (1.0 - sigma)))).astype(low)
        grad_up_low = (scaled * silu).astype(low)
        gated_low = (spread * hidden.astype(full)).astype(low)
        grad_rows = (
            matmul(grad_gate_low, gate_all, 1, 1) + matmul(grad_up_low, up_all, 1, 1)
        ).astype(low)
        saved.append((grad_gate_low, grad_up_low, gated_low, grad_rows))

    gate_send = jnp.stack(
        [g.reshape(expert_local, fsdp_size, rows).transpose(1, 0, 2) for g in gate_grads], axis=1
    )
    gate_back = lax.all_to_all(gate_send, "fsdp", split_axis=0, concat_axis=0, tiled=True)
    gate_sum = gate_back[:, 0] + pair_swap(gate_back[:, 1], 2)
    grad_prob = gate_sum.reshape(experts, rows).T

    grad_rows_own = scatter_plane(saved[0][3])
    grad_rows_pair = scatter_plane(saved[1][3])
    grad_from_rows = grad_rows_own.astype(full) + pair_swap(grad_rows_pair, 2).astype(full)

    grad_logits = (
        probs * (grad_prob - jnp.sum(probs * grad_prob, axis=-1, keepdims=True))
    ).astype(low)
    grad_router_t = matmul(grad_logits, ffn_normed, 0, 0)
    grad_ffn_normed = grad_from_rows + matmul(grad_logits, router_full, 1, 1)
    grad_scaled = grad_ffn_normed * ffn_gain_f
    grad_residual = (
        cotangent
        + ffn_scale * grad_scaled
        - residual
        * (ffn_scale * ffn_scale * ffn_scale)
        * jnp.mean(residual * grad_scaled, axis=-1, keepdims=True)
    )
    grad_ffn_gain_local = jnp.sum(grad_ffn_normed * residual * ffn_scale, axis=0)
    grad_attn = (row_keep * grad_residual).astype(low)
    grad_attn_all = line_gather(grad_attn)

    outs = [scatter_plane(matmul(saved[p][2], down_all, 1, 0).astype(low)) for p in range(2)]
    mixture = outs[0].astype(full) + pair_swap(outs[1], 2).astype(full)
    block_out = (residual + mixture).astype(low)

    def weight_grad(lefts, rights):
        total = matmul(lefts[0], rights[0], 0, 0)
        return total + matmul(lefts[1], rights[1], 0, 0)

    own_cols = expert_local * quarter
    gates_low = [saved[p][0] for p in range(2)]
    ups_low = [saved[p][1] for p in range(2)]
    gated = [saved[p][2] for p in range(2)]
    grad_gate_own = weight_grad(row_parts, [g[:, :own_cols] for g in gates_low])
    grad_up_own = weight_grad(row_parts, [g[:, :own_cols] for g in ups_low])
    grad_down_own = weight_grad([g[:, :own_cols] for g in gated], grad_parts)
    grad_gate_far = weight_grad(row_parts, [g[:, own_cols:] for g in gates_low]).astype(low)
    grad_up_far = weight_grad(row_parts, [g[:, own_cols:] for g in ups_low]).astype(low)
    grad_down_far = weight_grad([g[:, own_cols:] for g in gated], grad_parts).astype(low)
    grad_gate_sum = grad_gate_own + pair_swap(grad_gate_far, 1).astype(full)
    grad_up_sum = grad_up_own + pair_swap(grad_up_far, 1).astype(full)
    grad_down_sum = grad_down_own + pair_swap(grad_down_far, 1).astype(full)
    grad_w_gate = jnp.stack(
        [grad_gate_sum[:, e * quarter : (e + 1) * quarter] for e in range(expert_local)], axis=0
    )
    grad_w_up = jnp.stack(
        [grad_up_sum[:, e * quarter : (e + 1) * quarter] for e in range(expert_local)], axis=0
    )
    grad_w_down = grad_down_sum.reshape(expert_local, quarter, width)

    grad_mixed = matmul(grad_attn_all, w_out_t, 1, 0).astype(low)
    grad_output_t = matmul(grad_attn_all, mixed_out, 0, 0)
    grad_mixed_blocks = grad_mixed.reshape(block_count, block_rows, heads, HD)

    def backward_block(totals, block_in):
        key_total, value_total = totals
        query_block, grad_block, log_block = block_in
        scores = (
            jnp.einsum("qhd,khd->hqk", query_block, key_heads, preferred_element_type=full)
            * score_scale
        )
        scores = jnp.where(key_valid[None, None, :], scores, -1e30)
        attn_prob = jnp.exp(scores - log_block[..., None])
        prob_low = attn_prob.astype(low)
        value_total = value_total + jnp.einsum(
            "hqk,qhd->khd", prob_low, grad_block, preferred_element_type=full
        )
        grad_prob_block = jnp.einsum(
            "qhd,khd->hqk", grad_block, value_heads, preferred_element_type=full
        )
        row_delta = jnp.sum(attn_prob * grad_prob_block, axis=-1, keepdims=True)
        grad_scores = (attn_prob * (grad_prob_block - row_delta)).astype(low)
        grad_query_block = (
            jnp.einsum("hqk,khd->qhd", grad_scores, key_heads, preferred_element_type=full)
            * score_scale
        )
        key_total = (
            key_total
            + jnp.einsum("hqk,qhd->khd", grad_scores, query_block, preferred_element_type=full)
            * score_scale
        )
        return ((key_total, value_total), grad_query_block)

    zero_heads = jnp.zeros((group_rows, heads, HD), full)
    (grad_key, grad_value), grad_query_blocks = lax.scan(
        backward_block, (zero_heads, zero_heads), (query_blocks, grad_mixed_blocks, log_totals)
    )
    grad_query = grad_query_blocks.reshape(group_rows, heads * HD)
    prepare_fn = functools.partial(head_prepare, cos_table=cos_table, sin_table=sin_table)
    grad_query_pre, grad_query_gain_local = jax.vjp(prepare_fn, query_pre, query_gain_f)[1](
        grad_query
    )
    grad_key_pre, grad_key_gain_local = jax.vjp(prepare_fn, key_pre, key_gain_f)[1](
        grad_key.reshape(group_rows, heads * HD)
    )
    grad_qkv = jnp.concatenate(
        [
            grad_query_pre.astype(low),
            grad_key_pre.astype(low),
            grad_value.reshape(group_rows, heads * HD).astype(low),
        ],
        axis=1,
    )
    grad_normed_part = matmul(grad_qkv, w_qkv, 1, 1)
    grad_attn_gain_local = jnp.sum(grad_normed_part * group_full * row_scale, axis=0)
    grad_normed = line_scatter(
        [grad_normed_part[k * rows : (k + 1) * rows].astype(low) for k in range(tp_size)]
    )
    grad_scaled_in = grad_normed * attn_gain_f
    own_scale = row_scale[:rows]
    grad_input = grad_residual + (
        own_scale * grad_scaled_in
        - hidden_full
        * (own_scale * own_scale * own_scale)
        * jnp.mean(hidden_full * grad_scaled_in, axis=-1, keepdims=True)
    )

    grad_qkv_w = matmul(group_normed, grad_qkv, 0, 0)
    weight_pack = jnp.concatenate([grad_qkv_w.astype(low), grad_output_t.astype(low)], axis=1)
    weight_own = scatter_plane(weight_pack).astype(full)
    grad_w_query = weight_own[:, :head_width]
    grad_w_key = weight_own[:, head_width : 2 * head_width]
    grad_w_value = weight_own[:, 2 * head_width : 3 * head_width]
    grad_w_output = weight_own[:, 3 * head_width :].T

    both = ("fsdp", "tp")
    device = fsdp_place * tp_size + tp_place
    devices = fsdp_size * tp_size
    piece = width // devices
    gain_width = query_gain_f.shape[0]
    head_gains = jnp.zeros((width,), full)
    head_gains = head_gains.at[:gain_width].set(grad_query_gain_local)
    head_gains = head_gains.at[gain_width : 2 * gain_width].set(grad_key_gain_local)
    early = lax.psum(
        jnp.concatenate([grad_router_t, grad_ffn_gain_local[None, :]], axis=0), both
    )
    late = lax.psum(jnp.stack([grad_attn_gain_local, head_gains], axis=0), both)
    early_own = lax.dynamic_slice_in_dim(early, device * piece, piece, axis=1)
    grad_router = early_own[:experts].T
    grad_ffn_gain = early_own[experts]
    grad_attn_gain = lax.dynamic_slice_in_dim(late[0], device * piece, piece, axis=0)
    gain_own = gain_width // devices
    grad_query_gain = lax.dynamic_slice_in_dim(late[1], device * gain_own, gain_own, axis=0)
    grad_key_gain = lax.dynamic_slice_in_dim(
        late[1], gain_width + device * gain_own, gain_own, axis=0
    )
    return (
        block_out,
        grad_input,
        grad_attn_gain,
        grad_w_query,
        grad_w_key,
        grad_w_value,
        grad_query_gain,
        grad_key_gain,
        grad_w_output,
        grad_ffn_gain,
        grad_router,
        grad_w_gate,
        grad_w_up,
        grad_w_down,
    )


def per_device(*arrays):
    top_count = arrays[3].shape[1]
    experts = arrays[12].shape[1]
    if lax.axis_size("tp") == 4 and experts <= 2 * top_count:
        return per_device_dense(*arrays)
    return per_device_routed(*arrays)


def solution(mesh):
    return jax.shard_map(
        per_device,
        mesh=mesh,
        in_specs=(
            P(("fsdp", "tp"), None),
            P("fsdp"),
            P("fsdp"),
            P(("fsdp", "tp"), None),
            P("fsdp"),
            P("fsdp", "tp"),
            P("fsdp", "tp"),
            P("fsdp", "tp"),
            P("fsdp"),
            P("fsdp"),
            P("tp", "fsdp"),
            P("fsdp"),
            P("fsdp", None),
            P("fsdp", None, "tp"),
            P("fsdp", None, "tp"),
            P("fsdp", "tp", None),
            P(("fsdp", "tp"), None),
        ),
        out_specs=(
            P(("fsdp", "tp"), None),
            P(("fsdp", "tp"), None),
            P(("fsdp", "tp")),
            P("fsdp", "tp"),
            P("fsdp", "tp"),
            P("fsdp", "tp"),
            P(("fsdp", "tp")),
            P(("fsdp", "tp")),
            P("tp", "fsdp"),
            P(("fsdp", "tp")),
            P(("fsdp", "tp"), None),
            P("fsdp", None, "tp"),
            P("fsdp", None, "tp"),
            P("fsdp", "tp", None),
        ),
        check_vma=False,
    )
```
